32 devices in a mesh: gx: 4 (over y, core), gy: 8 (over z, x).
Axes of the slice: x: 2, y: 2, z: 4, core: 2. Of those that a mesh axis runs over, the one named last changes fastest.
Arguments:
- hidden: bfloat16 [128, 64, 4096], P(('gx', 'gy')), may hold values from -6 to 6
- parents: int32 [128, 64], P(('gx', 'gy')), may hold values from -1 to 62, as said below
- accepted: int32 [128, 64], P(('gx', 'gy')), may hold values 0 or 1
- token_ids: int32 [128, 64], P(('gx', 'gy')), may hold values from 0 to 128255
Outputs:
- dest_rows: bfloat16 [1024, 4096], P(('gx', 'gy'))
- accept_len: int32 [128], P(('gx', 'gy'))
- offsets: int32 [128], P(('gx', 'gy'))
- next_token: int32 [128], P(('gx', 'gy'))
The draws below stay inside these ranges and needn't reach their ends.
Inputs may be any that keep to these rules, and one draw needn't show every extreme that they name: parents[r, n] < n; node 0 is the only root; nodes 1 to 7 each have the previous node as parent; every node has depth at most 7.
All inputs are finite; a program needn't handle non-finite values. No bound on the sum of `accepted` on one device may be relied on, other than what follows from the above.
Results may differ from the reference program's by a relative error of at most 0.001.
Values may be sent and summed in bfloat16 or wider, within the bound.
A program may use at most 64 MiB of HBM per device.

```python
import math
import jax
import jax.numpy as jnp
import numpy as np
from jax import lax

D = 4096
NODES = 64
DEPTH = 8
BLOCK = 32
REQUESTS = 128
ROWS = 1024
N_GX = 4
N_GY = 8


def draw_parents(key, part):
    scores = jax.random.randint(jax.random.fold_in(key, 11), (REQUESTS, NODES, NODES), 0, 1048576)
    index = jnp.arange(NODES, dtype=jnp.int32)[None, :]

    def place(node, carry):
        parent_table, depth_table = carry
        valid = (index < node) & (depth_table < DEPTH - 1)
        ranked = jnp.where(valid, scores[:, node, :] * NODES + index, -1)
        chosen = jnp.argmax(ranked, axis=1).astype(jnp.int32)
        chosen = jnp.where(node < DEPTH, node - 1, chosen).astype(jnp.int32)
        level = jnp.where(node == 0, 0, jnp.take_along_axis(depth_table, jnp.maximum(chosen, 0)[:, None], axis=1)[:, 0] + 1)
        parent_table = parent_table.at[:, node].set(chosen)
        depth_table = depth_table.at[:, node].set(level.astype(jnp.int32))
        return (parent_table, depth_table)
    start = (jnp.full((REQUESTS, NODES), -1, jnp.int32), jnp.zeros((REQUESTS, NODES), jnp.int32))
    parent_table, depth_table = lax.fori_loop(0, NODES, place, start)
    return parent_table


def set_ends(result, stream_key, least, high):
    longest = result.shape.index(max(result.shape))
    spots = []
    for shift in (0, 1):
        where = [jax.random.randint(jax.random.fold_in(stream_key, axis), (), 0, length) for axis, length in enumerate(result.shape)]
        where[longest] = (where[longest] + shift) % result.shape[longest]
        spots.append(tuple(where))
    return result.at[spots[0]].set(least).at[spots[1]].set(high)


def block_scale(stream_key, shape, shards, smallest, high):
    def one(dim, shards_of):
        draws = jax.random.uniform(jax.random.fold_in(jax.random.fold_in(stream_key, 6), dim), (shards_of,), jnp.float32, smallest / len(shards), high / len(shards))
        return jnp.repeat(jnp.exp(draws), shape[dim] // shards_of).reshape((-1,) + (1,) * (len(shape) - dim - 1))

    level = one(*shards[0])
    for cut in shards[1:]:
        level = level * one(*cut)
    return level


def wide_ids(stream_key, shape, amount, lean):
    weights = [min(1 << octave, amount + 1 - (1 << octave)) * (1 << 20) // math.isqrt((1 << octave) ** lean) + 1 for octave in range((amount + 1).bit_length()) if 1 << octave <= amount]
    scale = 1 + sum(weights) // (1 << 30)
    grid = np.cumsum(np.array([max(1, weight // scale) for weight in weights]))
    ticket = jax.random.randint(jax.random.fold_in(stream_key, 1), shape, 0, int(grid[len(weights) - 1]))
    start = jnp.left_shift(1, jnp.searchsorted(jnp.asarray(grid, jnp.int32), ticket, side="right").astype(jnp.int32))
    grade = start - 1 + jax.random.randint(jax.random.fold_in(stream_key, 4), shape, 0, 1 << 30) % jnp.minimum(start, amount + 1 - start)
    return jax.random.permutation(jax.random.fold_in(stream_key, 2), amount)[grade].astype(jnp.int32)


def scatter_about(rng, dims, scale, reach, split=(), kind=jnp.bfloat16):
    array = jax.random.normal(rng, dims, jnp.float32) * scale
    if len(split) > 0:
        array = block_scale(rng, dims, split, -0.22, 0.18) * array
    return jnp.clip(array, min=-reach, max=reach).astype(kind)


def setup_inputs(seed: int = 0) -> dict:
    key_list = jax.random.split(jax.random.key(seed), 5)
    return {
        "hidden": scatter_about(key_list[0], (REQUESTS, NODES, D), 1.0, 6.0, ((0, 32),)),
        "parents": draw_parents(jax.random.fold_in(key_list[4], 71), 0),
        "accepted": set_ends((jax.random.randint(key_list[2], (REQUESTS, NODES), 0, 4) < 3).astype(jnp.int32), jax.random.fold_in(key_list[2], 1), 0, 1),
        "token_ids": set_ends(wide_ids(key_list[3], (REQUESTS, NODES), 128256, 2), jax.random.fold_in(key_list[3], 3), 0, 128255).astype(jnp.int32),
    }


def tree_walk(parents, accepted):
    nodes = parents.shape[1]
    index = jnp.arange(nodes, dtype=jnp.int32)[None, :]
    safe = jnp.maximum(parents, 0).astype(jnp.int32)
    is_root = parents < 0
    depth = jnp.zeros(parents.shape, jnp.int32)
    alive = jnp.ones(parents.shape, jnp.int32)
    for step in range(DEPTH):
        depth = jnp.where(is_root, 0, jnp.take_along_axis(depth, safe, axis=1) + 1).astype(jnp.int32)
        alive = jnp.where(is_root, 1, accepted * jnp.take_along_axis(alive, safe, axis=1)).astype(jnp.int32)
    score = jnp.where(alive == 1, depth * nodes + (nodes - 1 - index), -1)
    best = jnp.argmax(score, axis=1).astype(jnp.int32)
    length = (jnp.take_along_axis(depth, best[:, None], axis=1)[:, 0] + 1).astype(jnp.int32)
    on_path = jnp.zeros(parents.shape, jnp.bool_)
    current = best
    for step in range(DEPTH):
        on_path = on_path | ((index == current[:, None]) & (current[:, None] >= 0))
        upward = jnp.take_along_axis(parents, jnp.maximum(current, 0)[:, None].astype(jnp.int32), axis=1)[:, 0]
        current = jnp.where(current >= 0, upward, -1).astype(jnp.int32)
    return depth, on_path, best, length


def reference(hidden, parents, accepted, token_ids):
    depth, on_path, best, length = tree_walk(parents, accepted)
    offsets = (jnp.cumsum(length) - length).astype(jnp.int32)
    next_token = jnp.take_along_axis(token_ids, best[:, None], axis=1)[:, 0]
    target = jnp.where(on_path, offsets[:, None] + depth, ROWS).astype(jnp.int32)
    width = hidden.shape[2]
    packed = jnp.zeros((ROWS, width), jnp.bfloat16)
    packed = packed.at[target.reshape(-1)].set(hidden.reshape(-1, width), mode="drop")
    devices = N_GX * N_GY
    dest_rows = packed.reshape(BLOCK, devices, width).transpose(1, 0, 2).reshape(ROWS, width)
    return dest_rows, length, offsets, next_token
```

```python
import functools

import jax
import jax.numpy as jnp
from jax import lax
from jax.experimental import pallas as pl
from jax.experimental.pallas import tpu as pltpu
from jax.sharding import PartitionSpec as P

DEPTH = 8
FOLD = 16
MESH = pl.DeviceIdType.MESH


def mod(value, size):
    return value & (size - 1) if size & (size - 1) == 0 else lax.rem(value, size)


def div(value, size):
    if size & (size - 1) == 0:
        return lax.shift_right_logical(value, jnp.int32(size.bit_length() - 1) + jnp.zeros_like(value))
    return lax.div(value, jnp.int32(size) + jnp.zeros_like(value))


def lanes_of(table):
    return jnp.concatenate([table[r : r + 1, :] for r in range(table.shape[0])], axis=1)


def one_hot(rows, target):
    shape = (rows, target.shape[1])
    return (lax.broadcasted_iota(jnp.int32, shape, 0) == target).astype(jnp.bfloat16)


def kernel(
    sizes,
    hidden_ref,
    parents_ref,
    accepted_ref,
    tokens_ref,
    dest_ref,
    length_ref,
    offsets_ref,
    next_ref,
    hidden,
    staged,
    outgoing,
    incoming,
    count_out,
    counts,
    load_sem,
    own_sem,
    count_send,
    count_recv,
    row_send,
    row_recv,
):
    n_gx, n_gy, requests, nodes, width, block = sizes
    devices = n_gx * n_gy
    slab = width // FOLD
    every = requests * nodes
    me = lax.axis_index("gx") * n_gy + lax.axis_index("gy")

    def place(index):
        return (lax.div(index, n_gy), lax.rem(index, n_gy))

    def after(step):
        return lax.rem(me + step, devices)

    def ahead(step):
        return lax.rem(me + devices - step, devices)

    load = pltpu.make_async_copy(hidden_ref, hidden, load_sem)
    load.start()
    barrier = pltpu.get_barrier_semaphore()

    def greet(step, carry):
        pl.semaphore_signal(barrier, inc=1, device_id=place(after(step)), device_id_type=MESH)
        return carry

    lax.fori_loop(1, devices, greet, 0)

    lane = lax.broadcasted_iota(jnp.int32, (1, every), 1)
    group = div(lane, nodes)
    parents = lanes_of(parents_ref[...])
    bad = (parents >= 0) & (lanes_of(accepted_ref[...]) == 0)
    up = jnp.where(parents < 0, -1, parents + group * nodes)
    row = lax.broadcasted_iota(jnp.int32, (every, every), 0)
    col = lax.broadcasted_iota(jnp.int32, (every, every), 1)
    step_up = ((row == up) | (row == col)).astype(jnp.bfloat16)
    reach = step_up
    hops = 1
    while hops < DEPTH - 1:
        reach = jnp.dot(reach, reach, preferred_element_type=jnp.float32).astype(jnp.bfloat16)
        hops *= 2
    reach = (reach > 0).astype(jnp.bfloat16)
    which = lax.broadcasted_iota(jnp.int32, (16, every), 0)
    probe = jnp.where(which == 0, 1.0, jnp.where(bad, 1.0, 0.0)).astype(jnp.bfloat16)
    tally = jnp.dot(probe, reach, preferred_element_type=jnp.float32).astype(jnp.int32)
    depth = tally[0:1, :] - 1
    alive = tally[1:2, :] == 0
    score = jnp.where(alive, depth * nodes + (nodes - 1 - mod(lane, nodes)), -1)
    pad = 16
    mine = lax.broadcasted_iota(jnp.int32, (pad, every), 0) == group
    scores = jnp.where(mine, score, -1)
    top = jnp.max(scores.astype(jnp.float32), axis=1, keepdims=True).astype(jnp.int32)
    best_hot = mine & (scores == top)
    path = lax.dot_general(
        jnp.where(best_hot, 1.0, 0.0).astype(jnp.bfloat16),
        reach,
        (((1,), (1,)), ((), ())),
        preferred_element_type=jnp.float32,
    ).astype(jnp.int32)
    request = lax.broadcasted_iota(jnp.int32, (pad, 1), 0)
    length = jnp.where(request < requests, div(jnp.maximum(top, 0), nodes) + 1, 0)
    starts = []
    total = jnp.zeros((1, 1), jnp.int32)
    for r in range(requests):
        starts.append(total)
        total = total + length[r : r + 1, :]

    own_count = jnp.broadcast_to(total, (1, 128))
    count_out[0] = own_count
    counts[me] = own_count

    pl.semaphore_wait(barrier, devices - 1)

    def count_copy(step):
        return pltpu.make_async_remote_copy(
            src_ref=count_out.at[0],
            dst_ref=counts.at[me],
            send_sem=count_send.at[step],
            recv_sem=count_recv.at[me],
            device_id=place(after(step)),
            device_id_type=MESH,
        )

    def count_from(step):
        source = ahead(step)
        return pltpu.make_async_remote_copy(
            src_ref=count_out.at[0],
            dst_ref=counts.at[source],
            send_sem=count_send.at[step],
            recv_sem=count_recv.at[source],
            device_id=place(source),
            device_id_type=MESH,
        )

    def send_count(step, carry):
        count_copy(step).start()
        return carry

    lax.fori_loop(1, devices, send_count, 0)

    rank = jnp.where(jnp.sum(path.astype(jnp.float32), axis=0, keepdims=True) > 0, depth, -1)
    for r in range(requests):
        rank = jnp.where((group == r) & (rank >= 0), rank + starts[r], rank)
    load.wait()
    folded = jnp.zeros((block * FOLD, slab), jnp.float32)
    for piece in range(FOLD):
        take = one_hot(block * FOLD, jnp.where(rank >= 0, rank * FOLD + piece, -1))
        part = hidden[:, :, piece * slab : (piece + 1) * slab].reshape(every, slab)
        folded = folded + jnp.dot(take, part, preferred_element_type=jnp.float32)
    staged[0:block] = folded.astype(jnp.bfloat16).reshape(block, FOLD, slab)
    staged[block] = jnp.zeros((FOLD, slab), jnp.bfloat16)

    def await_count(step, carry):
        count_from(step).wait_recv()
        return carry

    lax.fori_loop(1, devices, await_count, 0)

    every_count = counts[...].reshape(devices, 128)
    source = lax.broadcasted_iota(jnp.int32, (devices, 128), 0)
    before_row = jnp.sum(jnp.where(source < me, every_count, 0).astype(jnp.float32), axis=0, keepdims=True)
    before_row = before_row.astype(jnp.int32)
    before = before_row[0, 0]

    for peer in range(devices):
        turn = mod(peer + devices * block * devices - before, devices)
        outgoing[peer] = staged[jnp.minimum(turn, block)]

    def row_copy(step):
        peer = after(step)
        return pltpu.make_async_remote_copy(
            src_ref=outgoing.at[peer],
            dst_ref=incoming.at[me],
            send_sem=row_send.at[step],
            recv_sem=row_recv.at[me],
            device_id=place(peer),
            device_id_type=MESH,
        )

    def row_from(step):
        origin = ahead(step)
        return pltpu.make_async_remote_copy(
            src_ref=outgoing.at[origin],
            dst_ref=incoming.at[origin],
            send_sem=row_send.at[step],
            recv_sem=row_recv.at[origin],
            device_id=place(origin),
            device_id_type=MESH,
        )

    def send_row(step, carry):
        row_copy(step).start()
        return carry

    lax.fori_loop(1, devices, send_row, 0)
    keep = pltpu.make_async_copy(outgoing.at[me], incoming.at[me], own_sem)
    keep.start()

    column = lax.broadcasted_iota(jnp.int32, (devices, devices * FOLD), 1)
    owner = lax.broadcasted_iota(jnp.int32, (devices, devices * FOLD), 0)
    wide = jnp.concatenate([every_count] * (devices * FOLD // 128), axis=1).astype(jnp.float32)
    of = div(column, FOLD)
    first = jnp.sum(jnp.where(owner < of, wide, 0.0), axis=0, keepdims=True).astype(jnp.int32)
    amount = jnp.sum(jnp.where(owner == of, wide, 0.0), axis=0, keepdims=True).astype(jnp.int32)
    turn = mod(me + devices * block * devices - first, devices)
    piece = mod(lax.broadcasted_iota(jnp.int32, (1, devices * FOLD), 1), FOLD)
    slot = div(first + turn, devices)
    placing = one_hot(block * FOLD, jnp.where(turn < amount, piece * block + slot, -1))

    tokens = lanes_of(tokens_ref[...])
    chosen = jnp.sum(jnp.where(best_hot, tokens, 0).astype(jnp.float32), axis=1, keepdims=True)
    chosen = chosen.astype(jnp.int32)
    for r in range(requests):
        length_ref[r] = length[r, 0]
        offsets_ref[r] = starts[r][0, 0] + before
        next_ref[r] = chosen[r, 0]

    keep.wait()

    def await_row(step, carry):
        row_from(step).wait_recv()
        return carry

    lax.fori_loop(1, devices, await_row, 0)
    rows = incoming[...].reshape(devices * FOLD, slab)
    placed = jnp.dot(placing, rows, preferred_element_type=jnp.float32).astype(jnp.bfloat16)
    for part in range(FOLD):
        dest_ref[:, part * slab : (part + 1) * slab] = placed[part * block : (part + 1) * block, :]

    def drain(step, carry):
        count_copy(step).wait_send()
        row_copy(step).wait_send()
        return carry

    lax.fori_loop(1, devices, drain, 0)


def solution(mesh):
    n_gx, n_gy = mesh.shape["gx"], mesh.shape["gy"]
    devices = n_gx * n_gy

    def local(hidden, parents, accepted, token_ids):
        requests, nodes, width = hidden.shape
        block = requests * DEPTH
        slab = width // FOLD
        vmem = pl.BlockSpec(memory_space=pltpu.VMEM)
        smem = pl.BlockSpec(memory_space=pltpu.SMEM)
        small = jax.ShapeDtypeStruct((requests,), jnp.int32)
        return pl.pallas_call(
            functools.partial(kernel, (n_gx, n_gy, requests, nodes, width, block)),
            out_shape=(jax.ShapeDtypeStruct((block, width), hidden.dtype), small, small, small),
            in_specs=[pl.BlockSpec(memory_space=pl.ANY), vmem, vmem, vmem],
            out_specs=(vmem, smem, smem, smem),
            scratch_shapes=[
                pltpu.VMEM(hidden.shape, hidden.dtype),
                pltpu.VMEM((block + 1, FOLD, slab), hidden.dtype),
                pltpu.VMEM((devices, FOLD, slab), hidden.dtype),
                pltpu.VMEM((devices, FOLD, slab), hidden.dtype),
                pltpu.VMEM((1, 1, 128), jnp.int32),
                pltpu.VMEM((devices, 1, 128), jnp.int32),
                pltpu.SemaphoreType.DMA,
                pltpu.SemaphoreType.DMA,
                pltpu.SemaphoreType.DMA((devices,)),
                pltpu.SemaphoreType.DMA((devices,)),
                pltpu.SemaphoreType.DMA((devices,)),
                pltpu.SemaphoreType.DMA((devices,)),
            ],
            compiler_params=pltpu.CompilerParams(collective_id=0, has_side_effects=True),
        )(hidden, parents, accepted, token_ids)

    placed = (
        P(("gx", "gy"), None, None),
        P(("gx", "gy"), None),
        P(("gx", "gy"), None),
        P(("gx", "gy"), None),
    )
    return jax.shard_map(
        local,
        mesh=mesh,
        in_specs=placed,
        out_specs=(P(("gx", "gy"), None), P(("gx", "gy")), P(("gx", "gy")), P(("gx", "gy"))),
        check_vma=False,
    )
```

```python
import functools

import jax
import jax.numpy as jnp
from jax import lax
from jax.experimental import pallas as pl
from jax.experimental.pallas import tpu as pltpu
from jax.sharding import PartitionSpec as P

DEPTH = 8
FOLD = 16
MESH = pl.DeviceIdType.MESH


def mod(value, size):
    return value & (size - 1) if size & (size - 1) == 0 else lax.rem(value, size)


def div(value, size):
    if size & (size - 1) == 0:
        return lax.shift_right_logical(value, jnp.int32(size.bit_length() - 1) + jnp.zeros_like(value))
    return lax.div(value, jnp.int32(size) + jnp.zeros_like(value))


def lanes_of(table):
    return jnp.concatenate([table[r : r + 1, :] for r in range(table.shape[0])], axis=1)


def one_hot(rows, target):
    shape = (rows, target.shape[1])
    return (lax.broadcasted_iota(jnp.int32, shape, 0) == target).astype(jnp.bfloat16)


def kernel(
    sizes,
    hidden_ref,
    parents_ref,
    accepted_ref,
    tokens_ref,
    dest_ref,
    length_ref,
    offsets_ref,
    next_ref,
    hidden,
    parents_in,
    accepted_in,
    tokens_in,
    staged,
    outgoing,
    incoming,
    count_out,
    near_counts,
    counts,
    load_sem,
    small_sem,
    own_sem,
    near_send,
    near_recv,
    far_send,
    far_recv,
    row_send,
    row_recv,
):
    n_gx, n_gy, requests, nodes, width, block = sizes
    devices = n_gx * n_gy
    slab = width // FOLD
    every = requests * nodes
    at_gx, at_gy = lax.axis_index("gx"), lax.axis_index("gy")
    me = at_gx * n_gy + at_gy
    near = [(lax.rem(at_gx + step, n_gx), at_gy) for step in range(1, n_gx)]
    far = [(at_gx, lax.rem(at_gy + step, n_gy)) for step in range(1, n_gy)]

    barrier = pltpu.get_barrier_semaphore()
    for partner in far + near:
        pl.semaphore_signal(barrier, inc=1, device_id=partner, device_id_type=MESH)
    loads = [
        pltpu.make_async_copy(parents_ref, parents_in, small_sem.at[0]),
        pltpu.make_async_copy(accepted_ref, accepted_in, small_sem.at[1]),
        pltpu.make_async_copy(tokens_ref, tokens_in, small_sem.at[2]),
        pltpu.make_async_copy(hidden_ref, hidden, load_sem),
    ]
    for load in loads:
        load.start()
    for load in loads[:3]:
        load.wait()

    lane = lax.broadcasted_iota(jnp.int32, (1, every), 1)
    group = div(lane, nodes)
    parents = lanes_of(parents_in[...])
    bad = (parents >= 0) & (lanes_of(accepted_in[...]) == 0)
    up = jnp.where(parents < 0, -1, parents + group * nodes)
    row = lax.broadcasted_iota(jnp.int32, (every, every), 0)
    col = lax.broadcasted_iota(jnp.int32, (every, every), 1)
    step_up = ((row == up) | (row == col)).astype(jnp.bfloat16)
    reach = step_up
    hops = 1
    while hops < DEPTH - 1:
        reach = jnp.dot(reach, reach, preferred_element_type=jnp.float32).astype(jnp.bfloat16)
        hops *= 2
    reach = (reach > 0).astype(jnp.bfloat16)
    which = lax.broadcasted_iota(jnp.int32, (16, every), 0)
    probe = jnp.where(which == 0, 1.0, jnp.where(bad, 1.0, 0.0)).astype(jnp.bfloat16)
    tally = jnp.dot(probe, reach, preferred_element_type=jnp.float32).astype(jnp.int32)
    depth = tally[0:1, :] - 1
    alive = tally[1:2, :] == 0
    score = jnp.where(alive, depth * nodes + (nodes - 1 - mod(lane, nodes)), -1)
    pad = 16
    mine = lax.broadcasted_iota(jnp.int32, (pad, every), 0) == group
    scores = jnp.where(mine, score, -1)
    top = jnp.max(scores.astype(jnp.float32), axis=1, keepdims=True).astype(jnp.int32)
    best_hot = mine & (scores == top)
    path = lax.dot_general(
        jnp.where(best_hot, 1.0, 0.0).astype(jnp.bfloat16),
        reach,
        (((1,), (1,)), ((), ())),
        preferred_element_type=jnp.float32,
    ).astype(jnp.int32)
    request = lax.broadcasted_iota(jnp.int32, (pad, 1), 0)
    length = jnp.where(request < requests, div(jnp.maximum(top, 0), nodes) + 1, 0)
    starts = []
    total = jnp.zeros((1, 1), jnp.int32)
    for r in range(requests):
        starts.append(total)
        total = total + length[r : r + 1, :]

    own_count = jnp.broadcast_to(total, (1, 128))
    count_out[0] = own_count
    near_counts[at_gx] = own_count

    pl.semaphore_wait(barrier, n_gx + n_gy - 2)

    near_copies = [
        pltpu.make_async_remote_copy(
            src_ref=count_out.at[0],
            dst_ref=near_counts.at[at_gx],
            send_sem=near_send,
            recv_sem=near_recv,
            device_id=partner,
            device_id_type=MESH,
        )
        for partner in near
    ]
    for copy in near_copies:
        copy.start()

    rank = jnp.where(jnp.sum(path.astype(jnp.float32), axis=0, keepdims=True) > 0, depth, -1)
    for r in range(requests):
        rank = jnp.where((group == r) & (rank >= 0), rank + starts[r], rank)
    def arrived(ref, amount, sem):
        part = ref.at[pl.ds(0, amount)]
        pltpu.make_async_copy(part, part, sem).wait()

    arrived(near_counts, n_gx - 1, near_recv)
    counts[at_gy] = near_counts[...]
    far_copies = [
        pltpu.make_async_remote_copy(
            src_ref=near_counts,
            dst_ref=counts.at[at_gy],
            send_sem=far_send,
            recv_sem=far_recv,
            device_id=partner,
            device_id_type=MESH,
        )
        for partner in far
    ]
    for copy in far_copies:
        copy.start()

    loads[3].wait()
    folded = jnp.zeros((block * FOLD, slab), jnp.float32)
    for piece in range(FOLD):
        take = one_hot(block * FOLD, jnp.where(rank >= 0, rank * FOLD + piece, -1))
        part = hidden[:, :, piece * slab : (piece + 1) * slab].reshape(every, slab)
        folded = folded + jnp.dot(take, part, preferred_element_type=jnp.float32)
    staged[0:block] = folded.astype(jnp.bfloat16).reshape(block, FOLD, slab)
    staged[block] = jnp.zeros((FOLD, slab), jnp.bfloat16)

    arrived(counts, n_gy - 1, far_recv)

    every_count = counts[...].reshape(devices, 128)

    def source_of(index):
        return mod(index, n_gx) * n_gy + div(index, n_gx)

    source = source_of(lax.broadcasted_iota(jnp.int32, (devices, 128), 0))
    before_row = jnp.sum(jnp.where(source < me, every_count, 0).astype(jnp.float32), axis=0, keepdims=True)
    before_row = before_row.astype(jnp.int32)
    before = before_row[0, 0]

    for peer in range(devices):
        turn = mod(peer + devices * block * devices - before, devices)
        outgoing[peer] = staged[jnp.minimum(turn, block)]

    row_copies = []
    for step in range(1, devices):
        peer = lax.rem(me + step, devices)
        row_copies.append(
            pltpu.make_async_remote_copy(
                src_ref=outgoing.at[peer],
                dst_ref=incoming.at[me],
                send_sem=row_send,
                recv_sem=row_recv,
                device_id=(lax.div(peer, n_gy), lax.rem(peer, n_gy)),
                device_id_type=MESH,
            )
        )
    for copy in row_copies:
        copy.start()
    keep = pltpu.make_async_copy(outgoing.at[me], incoming.at[me], own_sem)
    keep.start()

    column = lax.broadcasted_iota(jnp.int32, (devices, devices * FOLD), 1)
    owner = source_of(lax.broadcasted_iota(jnp.int32, (devices, devices * FOLD), 0))
    wide = jnp.concatenate([every_count] * (devices * FOLD // 128), axis=1).astype(jnp.float32)
    of = div(column, FOLD)
    first = jnp.sum(jnp.where(owner < of, wide, 0.0), axis=0, keepdims=True).astype(jnp.int32)
    amount = jnp.sum(jnp.where(owner == of, wide, 0.0), axis=0, keepdims=True).astype(jnp.int32)
    turn = mod(me + devices * block * devices - first, devices)
    piece = mod(lax.broadcasted_iota(jnp.int32, (1, devices * FOLD), 1), FOLD)
    slot = div(first + turn, devices)
    placing = one_hot(block * FOLD, jnp.where(turn < amount, piece * block + slot, -1))

    tokens = lanes_of(tokens_in[...])
    chosen = jnp.sum(jnp.where(best_hot, tokens, 0).astype(jnp.float32), axis=1, keepdims=True)
    chosen = chosen.astype(jnp.int32)
    for r in range(requests):
        length_ref[r] = length[r, 0]
        offsets_ref[r] = starts[r][0, 0] + before
        next_ref[r] = chosen[r, 0]

    keep.wait()

    arrived(incoming, devices - 1, row_recv)
    rows = incoming[...].reshape(devices * FOLD, slab)
    placed = jnp.dot(placing, rows, preferred_element_type=jnp.float32).astype(jnp.bfloat16)
    for part in range(FOLD):
        dest_ref[:, part * slab : (part + 1) * slab] = placed[part * block : (part + 1) * block, :]

    arrived(near_counts, n_gx - 1, near_send)
    arrived(counts, n_gy - 1, far_send)
    arrived(incoming, devices - 1, row_send)


def hand_on(*refs):
    half = (len(refs) - 1) // 2
    sems = refs[-1]
    copies = [pltpu.make_async_copy(refs[i], refs[half + i], sems.at[i]) for i in range(half)]
    for copy in copies:
        copy.start()
    for copy in copies:
        copy.wait()


def solution(mesh):
    n_gx, n_gy = mesh.shape["gx"], mesh.shape["gy"]
    devices = n_gx * n_gy

    def local(hidden, parents, accepted, token_ids):
        requests, nodes, width = hidden.shape
        block = requests * DEPTH
        slab = width // FOLD
        vmem = pl.BlockSpec(memory_space=pltpu.VMEM)
        smem = pl.BlockSpec(memory_space=pltpu.SMEM)
        small = jax.ShapeDtypeStruct((requests,), jnp.int32)
        anywhere = pl.BlockSpec(memory_space=pl.ANY)
        outs = (jax.ShapeDtypeStruct((block, width), hidden.dtype), small, small, small)
        results = pl.pallas_call(
            functools.partial(kernel, (n_gx, n_gy, requests, nodes, width, block)),
            out_shape=outs,
            in_specs=[pl.BlockSpec(memory_space=pltpu.HBM)] * 4,
            out_specs=(vmem, smem, smem, smem),
            scratch_shapes=[
                pltpu.VMEM(hidden.shape, hidden.dtype),
                pltpu.VMEM((requests, nodes), jnp.int32),
                pltpu.VMEM((requests, nodes), jnp.int32),
                pltpu.VMEM((requests, nodes), jnp.int32),
                pltpu.VMEM((block + 1, FOLD, slab), hidden.dtype),
                pltpu.VMEM((devices, FOLD, slab), hidden.dtype),
                pltpu.VMEM((devices, FOLD, slab), hidden.dtype),
                pltpu.VMEM((1, 1, 128), jnp.int32),
                pltpu.VMEM((n_gx, 1, 128), jnp.int32),
                pltpu.VMEM((n_gy, n_gx, 1, 128), jnp.int32),
                pltpu.SemaphoreType.DMA,
                pltpu.SemaphoreType.DMA((3,)),
                pltpu.SemaphoreType.DMA,
                pltpu.SemaphoreType.DMA,
                pltpu.SemaphoreType.DMA,
                pltpu.SemaphoreType.DMA,
                pltpu.SemaphoreType.DMA,
                pltpu.SemaphoreType.DMA,
                pltpu.SemaphoreType.DMA,
            ],
            compiler_params=pltpu.CompilerParams(
                collective_id=0, has_side_effects=True, vmem_limit_bytes=24 << 20
            ),
        )(hidden, parents, accepted, token_ids)
        return pl.pallas_call(
            hand_on,
            out_shape=outs,
            in_specs=[anywhere] * len(outs),
            out_specs=(anywhere,) * len(outs),
            scratch_shapes=[pltpu.SemaphoreType.DMA((len(outs),))],
            compiler_params=pltpu.CompilerParams(vmem_limit_bytes=1 << 20),
        )(*results)

    placed = (
        P(("gx", "gy"), None, None),
        P(("gx", "gy"), None),
        P(("gx", "gy"), None),
        P(("gx", "gy"), None),
    )
    return jax.shard_map(
        local,
        mesh=mesh,
        in_specs=placed,
        out_specs=(P(("gx", "gy"), None), P(("gx", "gy")), P(("gx", "gy")), P(("gx", "gy"))),
        check_vma=False,
    )
```

```python
import functools

import jax
import jax.numpy as jnp
from jax import lax
from jax.experimental import pallas as pl
from jax.experimental.pallas import tpu as pltpu
from jax.sharding import PartitionSpec as P

DEPTH = 8
FOLD = 16
MESH = pl.DeviceIdType.MESH


def mod(value, size):
    return value & (size - 1) if size & (size - 1) == 0 else lax.rem(value, size)


def div(value, size):
    if size & (size - 1) == 0:
        return lax.shift_right_logical(value, jnp.int32(size.bit_length() - 1) + jnp.zeros_like(value))
    return lax.div(value, jnp.int32(size) + jnp.zeros_like(value))


def lanes_of(table):
    return jnp.concatenate([table[r : r + 1, :] for r in range(table.shape[0])], axis=1)


def one_hot(rows, target):
    shape = (rows, target.shape[1])
    return (lax.broadcasted_iota(jnp.int32, shape, 0) == target).astype(jnp.bfloat16)


def kernel(
    sizes,
    hidden_ref,
    parents_ref,
    accepted_ref,
    tokens_ref,
    dest_ref,
    length_ref,
    offsets_ref,
    next_ref,
    hidden,
    parents_in,
    accepted_in,
    tokens_in,
    staged,
    outgoing,
    incoming,
    count_out,
    near_counts,
    counts,
    load_sem,
    small_sem,
    own_sem,
    near_send,
    near_recv,
    far_send,
    far_recv,
    row_send,
    row_recv,
):
    n_gx, n_gy, requests, nodes, width, block = sizes
    devices = n_gx * n_gy
    slab = width // FOLD
    every = requests * nodes
    at_gx, at_gy = lax.axis_index("gx"), lax.axis_index("gy")
    me = at_gx * n_gy + at_gy
    near = [(lax.rem(at_gx + step, n_gx), at_gy) for step in range(1, n_gx)]
    far = [(at_gx, lax.rem(at_gy + step, n_gy)) for step in range(1, n_gy)]

    barrier = pltpu.get_barrier_semaphore()
    for partner in far + near:
        pl.semaphore_signal(barrier, inc=1, device_id=partner, device_id_type=MESH)
    loads = [
        pltpu.make_async_copy(parents_ref, parents_in, small_sem.at[0]),
        pltpu.make_async_copy(accepted_ref, accepted_in, small_sem.at[1]),
        pltpu.make_async_copy(tokens_ref, tokens_in, small_sem.at[2]),
        pltpu.make_async_copy(hidden_ref, hidden, load_sem),
    ]
    for load in loads:
        load.start()
    for load in loads[:3]:
        load.wait()

    lane = lax.broadcasted_iota(jnp.int32, (1, every), 1)
    group = div(lane, nodes)
    parents = lanes_of(parents_in[...])
    bad = (parents >= 0) & (lanes_of(accepted_in[...]) == 0)
    up = jnp.where(parents < 0, -1, parents + group * nodes)
    row = lax.broadcasted_iota(jnp.int32, (every, every), 0)
    col = lax.broadcasted_iota(jnp.int32, (every, every), 1)
    step_up = ((row == up) | (row == col)).astype(jnp.bfloat16)
    reach = step_up
    hops = 1
    while hops < DEPTH - 1:
        reach = jnp.dot(reach, reach, preferred_element_type=jnp.float32).astype(jnp.bfloat16)
        hops *= 2
    reach = (reach > 0).astype(jnp.bfloat16)
    which = lax.broadcasted_iota(jnp.int32, (16, every), 0)
    probe = jnp.where(which == 0, 1.0, jnp.where(bad, 1.0, 0.0)).astype(jnp.bfloat16)
    tally = jnp.dot(probe, reach, preferred_element_type=jnp.float32).astype(jnp.int32)
    depth = tally[0:1, :] - 1
    alive = tally[1:2, :] == 0
    score = jnp.where(alive, depth * nodes + (nodes - 1 - mod(lane, nodes)), -1)
    pad = 16
    mine = lax.broadcasted_iota(jnp.int32, (pad, every), 0) == group
    scores = jnp.where(mine, score, -1)
    top = jnp.max(scores.astype(jnp.float32), axis=1, keepdims=True).astype(jnp.int32)
    best_hot = mine & (scores == top)
    path = lax.dot_general(
        jnp.where(best_hot, 1.0, 0.0).astype(jnp.bfloat16),
        reach,
        (((1,), (1,)), ((), ())),
        preferred_element_type=jnp.float32,
    ).astype(jnp.int32)
    request = lax.broadcasted_iota(jnp.int32, (pad, 1), 0)
    length = jnp.where(request < requests, div(jnp.maximum(top, 0), nodes) + 1, 0)
    starts = []
    total = jnp.zeros((1, 1), jnp.int32)
    for r in range(requests):
        starts.append(total)
        total = total + length[r : r + 1, :]

    own_count = jnp.broadcast_to(total, (1, 128))
    count_out[0] = own_count
    near_counts[at_gx] = own_count

    pl.semaphore_wait(barrier, n_gx + n_gy - 2)

    near_copies = [
        pltpu.make_async_remote_copy(
            src_ref=count_out.at[0],
            dst_ref=near_counts.at[at_gx],
            send_sem=near_send,
            recv_sem=near_recv,
            device_id=partner,
            device_id_type=MESH,
        )
        for partner in near
    ]
    for copy in near_copies:
        copy.start()

    rank = jnp.where(jnp.sum(path.astype(jnp.float32), axis=0, keepdims=True) > 0, depth, -1)
    for r in range(requests):
        rank = jnp.where((group == r) & (rank >= 0), rank + starts[r], rank)
    def arrived(ref, amount, sem):
        part = ref.at[pl.ds(0, amount)]
        pltpu.make_async_copy(part, part, sem).wait()

    arrived(near_counts, n_gx - 1, near_recv)
    counts[at_gy] = near_counts[...]
    far_copies = [
        pltpu.make_async_remote_copy(
            src_ref=near_counts,
            dst_ref=counts.at[at_gy],
            send_sem=far_send,
            recv_sem=far_recv,
            device_id=partner,
            device_id_type=MESH,
        )
        for partner in far
    ]
    for copy in far_copies:
        copy.start()

    loads[3].wait()
    folded = jnp.zeros((block * FOLD, slab), jnp.float32)
    for piece in range(FOLD):
        take = one_hot(block * FOLD, jnp.where(rank >= 0, rank * FOLD + piece, -1))
        part = hidden[:, :, piece * slab : (piece + 1) * slab].reshape(every, slab)
        folded = folded + jnp.dot(take, part, preferred_element_type=jnp.float32)
    staged[0:block] = folded.astype(jnp.bfloat16).reshape(block, FOLD, slab)
    staged[block] = jnp.zeros((FOLD, slab), jnp.bfloat16)

    arrived(counts, n_gy - 1, far_recv)

    every_count = counts[...].reshape(devices, 128)

    def source_of(index):
        return mod(index, n_gx) * n_gy + div(index, n_gx)

    source = source_of(lax.broadcasted_iota(jnp.int32, (devices, 128), 0))
    before_row = jnp.sum(jnp.where(source < me, every_count, 0).astype(jnp.float32), axis=0, keepdims=True)
    before_row = before_row.astype(jnp.int32)
    before = before_row[0, 0]

    for peer in range(devices):
        turn = mod(peer + devices * block * devices - before, devices)
        outgoing[peer] = staged[jnp.minimum(turn, block)]

    row_copies = []
    for step in range(1, devices):
        peer = lax.rem(me + step, devices)
        row_copies.append(
            pltpu.make_async_remote_copy(
                src_ref=outgoing.at[peer],
                dst_ref=incoming.at[me],
                send_sem=row_send,
                recv_sem=row_recv,
                device_id=(lax.div(peer, n_gy), lax.rem(peer, n_gy)),
                device_id_type=MESH,
            )
        )
    for copy in row_copies:
        copy.start()
    keep = pltpu.make_async_copy(outgoing.at[me], incoming.at[me], own_sem)
    keep.start()

    column = lax.broadcasted_iota(jnp.int32, (devices, devices * FOLD), 1)
    owner = source_of(lax.broadcasted_iota(jnp.int32, (devices, devices * FOLD), 0))
    wide = jnp.concatenate([every_count] * (devices * FOLD // 128), axis=1).astype(jnp.float32)
    of = div(column, FOLD)
    first = jnp.sum(jnp.where(owner < of, wide, 0.0), axis=0, keepdims=True).astype(jnp.int32)
    amount = jnp.sum(jnp.where(owner == of, wide, 0.0), axis=0, keepdims=True).astype(jnp.int32)
    turn = mod(me + devices * block * devices - first, devices)
    piece = mod(lax.broadcasted_iota(jnp.int32, (1, devices * FOLD), 1), FOLD)
    slot = div(first + turn, devices)
    placing = one_hot(block * FOLD, jnp.where(turn < amount, piece * block + slot, -1))

    tokens = lanes_of(tokens_in[...])
    chosen = jnp.sum(jnp.where(best_hot, tokens, 0).astype(jnp.float32), axis=1, keepdims=True)
    chosen = chosen.astype(jnp.int32)
    for r in range(requests):
        length_ref[r] = length[r, 0]
        offsets_ref[r] = starts[r][0, 0] + before
        next_ref[r] = chosen[r, 0]

    keep.wait()

    arrived(incoming, devices - 1, row_recv)
    rows = incoming[...].reshape(devices * FOLD, slab)
    placed = jnp.dot(placing, rows, preferred_element_type=jnp.float32).astype(jnp.bfloat16)
    for part in range(FOLD):
        dest_ref[:, part * slab : (part + 1) * slab] = placed[part * block : (part + 1) * block, :]

    arrived(near_counts, n_gx - 1, near_send)
    arrived(counts, n_gy - 1, far_send)
    arrived(incoming, devices - 1, row_send)


def hand_on(*refs):
    half = (len(refs) - 1) // 2
    sems = refs[-1]
    copies = [pltpu.make_async_copy(refs[i], refs[half + i], sems.at[i]) for i in range(half)]
    for copy in copies:
        copy.start()
    for copy in copies:
        copy.wait()


def solution(mesh):
    n_gx, n_gy = mesh.shape["gx"], mesh.shape["gy"]
    devices = n_gx * n_gy

    def local(hidden, parents, accepted, token_ids):
        requests, nodes, width = hidden.shape
        block = requests * DEPTH
        slab = width // FOLD
        vmem = pl.BlockSpec(memory_space=pltpu.VMEM)
        smem = pl.BlockSpec(memory_space=pltpu.SMEM)
        small = jax.ShapeDtypeStruct((requests,), jnp.int32)
        anywhere = pl.BlockSpec(memory_space=pl.ANY)
        outs = (jax.ShapeDtypeStruct((block, width), hidden.dtype), small, small, small)
        results = pl.pallas_call(
            functools.partial(kernel, (n_gx, n_gy, requests, nodes, width, block)),
            out_shape=outs,
            in_specs=[pl.BlockSpec(memory_space=pltpu.HBM)] * 4,
            out_specs=(vmem, smem, smem, smem),
            scratch_shapes=[
                pltpu.VMEM(hidden.shape, hidden.dtype),
                pltpu.VMEM((requests, nodes), jnp.int32),
                pltpu.VMEM((requests, nodes), jnp.int32),
                pltpu.VMEM((requests, nodes), jnp.int32),
                pltpu.VMEM((block + 1, FOLD, slab), hidden.dtype),
                pltpu.VMEM((devices, FOLD, slab), hidden.dtype),
                pltpu.VMEM((devices, FOLD, slab), hidden.dtype),
                pltpu.VMEM((1, 1, 128), jnp.int32),
                pltpu.VMEM((n_gx, 1, 128), jnp.int32),
                pltpu.VMEM((n_gy, n_gx, 1, 128), jnp.int32),
                pltpu.SemaphoreType.DMA,
                pltpu.SemaphoreType.DMA((3,)),
                pltpu.SemaphoreType.DMA,
                pltpu.SemaphoreType.DMA,
                pltpu.SemaphoreType.DMA,
                pltpu.SemaphoreType.DMA,
                pltpu.SemaphoreType.DMA,
                pltpu.SemaphoreType.DMA,
                pltpu.SemaphoreType.DMA,
            ],
            compiler_params=pltpu.CompilerParams(
                collective_id=0, has_side_effects=True, vmem_limit_bytes=24 << 20
            ),
        )(*[pltpu.with_memory_space_constraint(x, pltpu.HBM) for x in (hidden, parents, accepted, token_ids)])
        return pl.pallas_call(
            hand_on,
            out_shape=outs,
            in_specs=[anywhere] * len(outs),
            out_specs=(anywhere,) * len(outs),
            scratch_shapes=[pltpu.SemaphoreType.DMA((len(outs),))],
            compiler_params=pltpu.CompilerParams(vmem_limit_bytes=1 << 20),
        )(*results)

    placed = (
        P(("gx", "gy"), None, None),
        P(("gx", "gy"), None),
        P(("gx", "gy"), None),
        P(("gx", "gy"), None),
    )
    return jax.shard_map(
        local,
        mesh=mesh,
        in_specs=placed,
        out_specs=(P(("gx", "gy"), None), P(("gx", "gy")), P(("gx", "gy")), P(("gx", "gy"))),
        check_vma=False,
    )
```

```python
import functools

import jax
import jax.numpy as jnp
from jax import lax
from jax.experimental import pallas as pl
from jax.experimental.pallas import tpu as pltpu
from jax.sharding import PartitionSpec as P

DEPTH = 8
FOLD = 16
MESH = pl.DeviceIdType.MESH


def mod(value, size):
    return value & (size - 1) if size & (size - 1) == 0 else lax.rem(value, size)


def div(value, size):
    if size & (size - 1) == 0:
        return lax.shift_right_logical(value, jnp.int32(size.bit_length() - 1) + jnp.zeros_like(value))
    return lax.div(value, jnp.int32(size) + jnp.zeros_like(value))


def lanes_of(table):
    return jnp.concatenate([table[r : r + 1, :] for r in range(table.shape[0])], axis=1)


def one_hot(rows, target):
    shape = (rows, target.shape[1])
    return (lax.broadcasted_iota(jnp.int32, shape, 0) == target).astype(jnp.bfloat16)


def kernel(
    sizes,
    hidden_ref,
    parents_ref,
    accepted_ref,
    tokens_ref,
    dest_ref,
    length_ref,
    offsets_ref,
    next_ref,
    hidden,
    parents_in,
    accepted_in,
    tokens_in,
    staged,
    outgoing,
    incoming,
    count_out,
    counts,
    load_sem,
    small_sem,
    own_sem,
    count_send,
    count_recv,
    row_send,
    row_recv,
):
    n_gx, n_gy, requests, nodes, width, block = sizes
    devices = n_gx * n_gy
    slab = width // FOLD
    every = requests * nodes
    me = lax.axis_index("gx") * n_gy + lax.axis_index("gy")

    def others(order):
        if devices & (devices - 1):
            return [lax.rem(me + step, devices) for step in order]
        return [me ^ step for step in order]

    def place(index):
        return (div(index, n_gy), mod(index, n_gy))

    barrier = pltpu.get_barrier_semaphore()
    for peer in others(range(devices - 1, 0, -1)):
        pl.semaphore_signal(barrier, inc=1, device_id=place(peer), device_id_type=MESH)
    loads = [
        pltpu.make_async_copy(parents_ref, parents_in, small_sem.at[0]),
        pltpu.make_async_copy(accepted_ref, accepted_in, small_sem.at[1]),
        pltpu.make_async_copy(tokens_ref, tokens_in, small_sem.at[2]),
        pltpu.make_async_copy(hidden_ref, hidden, load_sem),
    ]
    for load in loads:
        load.start()
    for load in loads[:3]:
        load.wait()

    def padded(table, fill):
        wide = jnp.concatenate([table, jnp.full((requests, 128 - nodes), fill, jnp.int32)], axis=1)
        return jnp.concatenate([wide, jnp.full((8 - requests, 128), fill, jnp.int32)], axis=0)

    parents = padded(parents_in[...], -1)
    accepted = padded(accepted_in[...], 1)
    at_node = lax.broadcasted_iota(jnp.int32, (8, 128), 1)
    request = lax.broadcasted_iota(jnp.int32, (8, 128), 0)
    jump = jnp.where(parents < 0, at_node, parents)
    tally = jnp.where(parents < 0, 0, jnp.where(accepted == 0, nodes + 1, 1))
    hops = 1
    while hops < DEPTH - 1:
        tally = tally + jnp.take_along_axis(tally, jump, axis=1, mode="promise_in_bounds")
        hops *= 2
        if hops < DEPTH - 1:
            jump = jnp.take_along_axis(jump, jump, axis=1, mode="promise_in_bounds")
    real = (at_node < nodes) & (request < requests)
    level = mod(tally, nodes)
    score = jnp.where(real & (tally < nodes), level * nodes + (nodes - 1 - at_node), -1)
    top = jnp.max(score.astype(jnp.float32), axis=1, keepdims=True).astype(jnp.int32)
    length = jnp.where(top >= 0, div(jnp.maximum(top, 0), nodes) + 1, 0)
    starts = []
    total = jnp.zeros((1, 1), jnp.int32)
    for r in range(requests):
        starts.append(total)
        total = total + length[r : r + 1, :]

    own_count = jnp.broadcast_to(total, (1, 128))
    count_out[0] = own_count
    counts[me] = own_count

    pl.semaphore_wait(barrier, devices - 1)

    count_copies = [
        pltpu.make_async_remote_copy(
            src_ref=count_out.at[0],
            dst_ref=counts.at[me],
            send_sem=count_send,
            recv_sem=count_recv,
            device_id=place(peer),
            device_id_type=MESH,
        )
        for peer in others(range(devices - 1, 0, -1))
    ]
    for copy in count_copies:
        copy.start()

    lane = lax.broadcasted_iota(jnp.int32, (1, every), 1)
    group = div(lane, nodes)
    above = lanes_of(parents_in[...])
    up = jnp.where(above < 0, -1, above + group * nodes)
    row = lax.broadcasted_iota(jnp.int32, (every, every), 0)
    col = lax.broadcasted_iota(jnp.int32, (every, every), 1)
    reach = ((row == up) | (row == col)).astype(jnp.bfloat16)
    hops = 1
    while hops < DEPTH - 1:
        reach = jnp.dot(reach, reach, preferred_element_type=jnp.float32).astype(jnp.bfloat16)
        hops *= 2
    reach = (reach > 0).astype(jnp.bfloat16)
    best = nodes - 1 - mod(jnp.maximum(top, 0), nodes)
    ends = (lane == best + request[:, 0:1] * nodes) & (top >= 0)
    ends = jnp.concatenate([ends.astype(jnp.float32), jnp.zeros((8, every), jnp.float32)], axis=0)
    path = lax.dot_general(
        ends.astype(jnp.bfloat16), reach, (((1,), (1,)), ((), ())), preferred_element_type=jnp.float32
    )
    depth = lanes_of(level[0:requests, 0:nodes])

    rank = jnp.where(jnp.sum(path, axis=0, keepdims=True) > 0, depth, -1)
    for r in range(requests):
        rank = jnp.where((group == r) & (rank >= 0), rank + starts[r], rank)
    def arrived(ref, amount, sem):
        part = ref.at[pl.ds(0, amount)]
        pltpu.make_async_copy(part, part, sem).wait()

    loads[3].wait()
    folded = jnp.zeros((block * FOLD, slab), jnp.float32)
    for piece in range(FOLD):
        take = one_hot(block * FOLD, jnp.where(rank >= 0, rank * FOLD + piece, -1))
        part = hidden[:, :, piece * slab : (piece + 1) * slab].reshape(every, slab)
        folded = folded + jnp.dot(take, part, preferred_element_type=jnp.float32)
    staged[0:block] = folded.astype(jnp.bfloat16).reshape(block, FOLD, slab)
    staged[block] = jnp.zeros((FOLD, slab), jnp.bfloat16)

    arrived(counts, devices - 1, count_recv)

    every_count = counts[...].reshape(devices, 128)
    source = lax.broadcasted_iota(jnp.int32, (devices, 128), 0)
    before_row = jnp.sum(jnp.where(source < me, every_count, 0).astype(jnp.float32), axis=0, keepdims=True)
    before_row = before_row.astype(jnp.int32)
    before = before_row[0, 0]

    for peer in range(devices):
        turn = mod(peer + devices * block * devices - before, devices)
        outgoing[peer] = staged[jnp.minimum(turn, block)]

    row_copies = [
        pltpu.make_async_remote_copy(
            src_ref=outgoing.at[peer],
            dst_ref=incoming.at[me],
            send_sem=row_send,
            recv_sem=row_recv,
            device_id=place(peer),
            device_id_type=MESH,
        )
        for peer in others(range(1, devices))
    ]
    for copy in row_copies:
        copy.start()
    keep = pltpu.make_async_copy(outgoing.at[me], incoming.at[me], own_sem)
    keep.start()

    column = lax.broadcasted_iota(jnp.int32, (devices, devices * FOLD), 1)
    owner = lax.broadcasted_iota(jnp.int32, (devices, devices * FOLD), 0)
    wide = jnp.concatenate([every_count] * (devices * FOLD // 128), axis=1).astype(jnp.float32)
    of = div(column, FOLD)
    first = jnp.sum(jnp.where(owner < of, wide, 0.0), axis=0, keepdims=True).astype(jnp.int32)
    amount = jnp.sum(jnp.where(owner == of, wide, 0.0), axis=0, keepdims=True).astype(jnp.int32)
    turn = mod(me + devices * block * devices - first, devices)
    piece = mod(lax.broadcasted_iota(jnp.int32, (1, devices * FOLD), 1), FOLD)
    slot = div(first + turn, devices)
    placing = one_hot(block * FOLD, jnp.where(turn < amount, piece * block + slot, -1))

    chosen = jnp.where(score == top, padded(tokens_in[...], 0), 0).astype(jnp.float32)
    chosen = jnp.sum(chosen, axis=1, keepdims=True)
    chosen = chosen.astype(jnp.int32)
    for r in range(requests):
        length_ref[r] = length[r, 0]
        offsets_ref[r] = starts[r][0, 0] + before
        next_ref[r] = chosen[r, 0]

    keep.wait()

    arrived(incoming, devices - 1, row_recv)
    rows = incoming[...].reshape(devices * FOLD, slab)
    placed = jnp.dot(placing, rows, preferred_element_type=jnp.float32).astype(jnp.bfloat16)
    for part in range(FOLD):
        dest_ref[:, part * slab : (part + 1) * slab] = placed[part * block : (part + 1) * block, :]

    arrived(counts, devices - 1, count_send)
    arrived(incoming, devices - 1, row_send)


def hand_on(*refs):
    half = (len(refs) - 1) // 2
    sems = refs[-1]
    copies = [pltpu.make_async_copy(refs[i], refs[half + i], sems.at[i]) for i in range(half)]
    for copy in copies:
        copy.start()
    for copy in copies:
        copy.wait()


def solution(mesh):
    n_gx, n_gy = mesh.shape["gx"], mesh.shape["gy"]
    devices = n_gx * n_gy

    def local(hidden, parents, accepted, token_ids):
        requests, nodes, width = hidden.shape
        block = requests * DEPTH
        slab = width // FOLD
        vmem = pl.BlockSpec(memory_space=pltpu.VMEM)
        smem = pl.BlockSpec(memory_space=pltpu.SMEM)
        small = jax.ShapeDtypeStruct((requests,), jnp.int32)
        anywhere = pl.BlockSpec(memory_space=pl.ANY)
        outs = (jax.ShapeDtypeStruct((block, width), hidden.dtype), small, small, small)
        results = pl.pallas_call(
            functools.partial(kernel, (n_gx, n_gy, requests, nodes, width, block)),
            out_shape=outs,
            in_specs=[pl.BlockSpec(memory_space=pltpu.HBM)] * 4,
            out_specs=(vmem, smem, smem, smem),
            scratch_shapes=[
                pltpu.VMEM(hidden.shape, hidden.dtype),
                pltpu.VMEM((requests, nodes), jnp.int32),
                pltpu.VMEM((requests, nodes), jnp.int32),
                pltpu.VMEM((requests, nodes), jnp.int32),
                pltpu.VMEM((block + 1, FOLD, slab), hidden.dtype),
                pltpu.VMEM((devices, FOLD, slab), hidden.dtype),
                pltpu.VMEM((devices, FOLD, slab), hidden.dtype),
                pltpu.VMEM((1, 1, 128), jnp.int32),
                pltpu.VMEM((devices, 1, 128), jnp.int32),
                pltpu.SemaphoreType.DMA,
                pltpu.SemaphoreType.DMA((3,)),
                pltpu.SemaphoreType.DMA,
                pltpu.SemaphoreType.DMA,
                pltpu.SemaphoreType.DMA,
                pltpu.SemaphoreType.DMA,
                pltpu.SemaphoreType.DMA,
            ],
            compiler_params=pltpu.CompilerParams(
                collective_id=0, has_side_effects=True, vmem_limit_bytes=24 << 20
            ),
        )(*[pltpu.with_memory_space_constraint(x, pltpu.HBM) for x in (hidden, parents, accepted, token_ids)])
        return pl.pallas_call(
            hand_on,
            out_shape=outs,
            in_specs=[anywhere] * len(outs),
            out_specs=(anywhere,) * len(outs),
            scratch_shapes=[pltpu.SemaphoreType.DMA((len(outs),))],
            compiler_params=pltpu.CompilerParams(vmem_limit_bytes=1 << 20),
        )(*results)

    placed = (
        P(("gx", "gy"), None, None),
        P(("gx", "gy"), None),
        P(("gx", "gy"), None),
        P(("gx", "gy"), None),
    )
    return jax.shard_map(
        local,
        mesh=mesh,
        in_specs=placed,
        out_specs=(P(("gx", "gy"), None), P(("gx", "gy")), P(("gx", "gy")), P(("gx", "gy"))),
        check_vma=False,
    )
```

```python
import functools

import jax
import jax.numpy as jnp
from jax import lax
from jax.experimental import pallas as pl
from jax.experimental.pallas import tpu as pltpu
from jax.sharding import PartitionSpec as P

DEPTH = 8
FOLD = 16
MESH = pl.DeviceIdType.MESH


def mod(value, size):
    return value & (size - 1) if size & (size - 1) == 0 else lax.rem(value, size)


def div(value, size):
    if size & (size - 1) == 0:
        return lax.shift_right_logical(value, jnp.int32(size.bit_length() - 1) + jnp.zeros_like(value))
    return lax.div(value, jnp.int32(size) + jnp.zeros_like(value))


def lanes_of(table):
    return jnp.concatenate([table[r : r + 1, :] for r in range(table.shape[0])], axis=1)


def one_hot(rows, target):
    shape = (rows, target.shape[1])
    return (lax.broadcasted_iota(jnp.int32, shape, 0) == target).astype(jnp.bfloat16)


def kernel(
    sizes,
    hidden_ref,
    parents_ref,
    accepted_ref,
    tokens_ref,
    dest_ref,
    length_ref,
    offsets_ref,
    next_ref,
    hidden,
    parents_in,
    accepted_in,
    tokens_in,
    staged,
    outgoing,
    incoming,
    count_out,
    counts,
    load_sem,
    small_sem,
    own_sem,
    count_send,
    count_recv,
    row_send,
    row_recv,
):
    n_gx, n_gy, requests, nodes, width, block = sizes
    devices = n_gx * n_gy
    slab = width // FOLD
    every = requests * nodes
    me = lax.axis_index("gx") * n_gy + lax.axis_index("gy")

    def others(order):
        if devices & (devices - 1):
            return [lax.rem(me + step, devices) for step in order]
        return [me ^ step for step in order]

    def place(index):
        return (div(index, n_gy), mod(index, n_gy))

    barrier = pltpu.get_barrier_semaphore()
    for peer in others(range(devices - 1, 0, -1)):
        pl.semaphore_signal(barrier, inc=1, device_id=place(peer), device_id_type=MESH)
    loads = [
        pltpu.make_async_copy(parents_ref, parents_in, small_sem.at[0]),
        pltpu.make_async_copy(accepted_ref, accepted_in, small_sem.at[1]),
        pltpu.make_async_copy(tokens_ref, tokens_in, small_sem.at[2]),
        pltpu.make_async_copy(hidden_ref, hidden, load_sem),
    ]
    for load in loads:
        load.start()
    for load in loads[:3]:
        load.wait()

    def padded(table, fill):
        wide = jnp.concatenate([table, jnp.full((requests, 128 - nodes), fill, jnp.int32)], axis=1)
        return jnp.concatenate([wide, jnp.full((8 - requests, 128), fill, jnp.int32)], axis=0)

    parents = padded(parents_in[...], -1)
    accepted = padded(accepted_in[...], 1)
    at_node = lax.broadcasted_iota(jnp.int32, (8, 128), 1)
    request = lax.broadcasted_iota(jnp.int32, (8, 128), 0)
    jump = jnp.where(parents < 0, at_node, parents)
    tally = jnp.where(parents < 0, 0, jnp.where(accepted == 0, nodes + 1, 1))
    hops = 1
    while hops < DEPTH - 1:
        tally = tally + jnp.take_along_axis(tally, jump, axis=1, mode="promise_in_bounds")
        hops *= 2
        if hops < DEPTH - 1:
            jump = jnp.take_along_axis(jump, jump, axis=1, mode="promise_in_bounds")
    real = (at_node < nodes) & (request < requests)
    level = mod(tally, nodes)
    score = jnp.where(real & (tally < nodes), level * nodes + (nodes - 1 - at_node), -1)
    top = jnp.max(score.astype(jnp.float32), axis=1, keepdims=True).astype(jnp.int32)
    length = jnp.where(top >= 0, div(jnp.maximum(top, 0), nodes) + 1, 0)
    starts = []
    total = jnp.zeros((1, 1), jnp.int32)
    for r in range(requests):
        starts.append(total)
        total = total + length[r : r + 1, :]

    own_count = jnp.broadcast_to(total, (1, 128))
    count_out[0] = own_count
    counts[me] = own_count

    pl.semaphore_wait(barrier, devices - 1)

    count_copies = [
        pltpu.make_async_remote_copy(
            src_ref=count_out.at[0],
            dst_ref=counts.at[me],
            send_sem=count_send,
            recv_sem=count_recv,
            device_id=place(peer),
            device_id_type=MESH,
        )
        for peer in others(range(devices - 1, 0, -1))
    ]
    for copy in count_copies:
        copy.start()

    lane = lax.broadcasted_iota(jnp.int32, (1, every), 1)
    group = div(lane, nodes)
    above = lanes_of(parents_in[...])
    up = jnp.where(above < 0, -1, above + group * nodes)
    row = lax.broadcasted_iota(jnp.int32, (every, every), 0)
    col = lax.broadcasted_iota(jnp.int32, (every, every), 1)
    reach = ((row == up) | (row == col)).astype(jnp.bfloat16)
    hops = 1
    while hops < DEPTH - 1:
        reach = jnp.dot(reach, reach, preferred_element_type=jnp.float32).astype(jnp.bfloat16)
        hops *= 2
    reach = (reach > 0).astype(jnp.bfloat16)
    best = nodes - 1 - mod(jnp.maximum(top, 0), nodes)
    ends = (lane == best + request[:, 0:1] * nodes) & (top >= 0)
    ends = jnp.concatenate([ends.astype(jnp.float32), jnp.zeros((8, every), jnp.float32)], axis=0)
    path = lax.dot_general(
        ends.astype(jnp.bfloat16), reach, (((1,), (1,)), ((), ())), preferred_element_type=jnp.float32
    )
    depth = lanes_of(level[0:requests, 0:nodes])

    rank = jnp.where(jnp.sum(path, axis=0, keepdims=True) > 0, depth, -1)
    for r in range(requests):
        rank = jnp.where((group == r) & (rank >= 0), rank + starts[r], rank)
    def arrived(ref, amount, sem):
        part = ref.at[pl.ds(0, amount)]
        pltpu.make_async_copy(part, part, sem).wait()

    loads[3].wait()
    folded = jnp.zeros((block * FOLD, slab), jnp.float32)
    for piece in range(FOLD):
        take = one_hot(block * FOLD, jnp.where(rank >= 0, rank * FOLD + piece, -1))
        part = hidden[:, :, piece * slab : (piece + 1) * slab].reshape(every, slab)
        folded = folded + jnp.dot(take, part, preferred_element_type=jnp.float32)
    staged[0:block] = folded.astype(jnp.bfloat16).reshape(block, FOLD, slab)
    staged[block] = jnp.zeros((FOLD, slab), jnp.bfloat16)

    arrived(counts, devices - 1, count_recv)

    every_count = counts[...].reshape(devices, 128)
    source = lax.broadcasted_iota(jnp.int32, (devices, 128), 0)
    before_row = jnp.sum(jnp.where(source < me, every_count, 0).astype(jnp.float32), axis=0, keepdims=True)
    before_row = before_row.astype(jnp.int32)
    before = before_row[0, 0]

    for peer in range(devices):
        turn = mod(peer + devices * block * devices - before, devices)
        outgoing[peer] = staged[jnp.minimum(turn, block)]

    ring = n_gy // 2

    def reach_of(step):
        turn = step % n_gy // 2
        return (-min(turn, ring - turn), -turn, -step)

    far_first = sorted(range(1, devices), key=reach_of)
    row_copies = [
        pltpu.make_async_remote_copy(
            src_ref=outgoing.at[peer],
            dst_ref=incoming.at[me],
            send_sem=row_send,
            recv_sem=row_recv,
            device_id=place(peer),
            device_id_type=MESH,
        )
        for peer in others(far_first)
    ]
    for copy in row_copies:
        copy.start()
    keep = pltpu.make_async_copy(outgoing.at[me], incoming.at[me], own_sem)
    keep.start()

    column = lax.broadcasted_iota(jnp.int32, (devices, devices * FOLD), 1)
    owner = lax.broadcasted_iota(jnp.int32, (devices, devices * FOLD), 0)
    wide = jnp.concatenate([every_count] * (devices * FOLD // 128), axis=1).astype(jnp.float32)
    of = div(column, FOLD)
    first = jnp.sum(jnp.where(owner < of, wide, 0.0), axis=0, keepdims=True).astype(jnp.int32)
    amount = jnp.sum(jnp.where(owner == of, wide, 0.0), axis=0, keepdims=True).astype(jnp.int32)
    turn = mod(me + devices * block * devices - first, devices)
    piece = mod(lax.broadcasted_iota(jnp.int32, (1, devices * FOLD), 1), FOLD)
    slot = div(first + turn, devices)
    placing = one_hot(block * FOLD, jnp.where(turn < amount, piece * block + slot, -1))

    chosen = jnp.where(score == top, padded(tokens_in[...], 0), 0).astype(jnp.float32)
    chosen = jnp.sum(chosen, axis=1, keepdims=True)
    chosen = chosen.astype(jnp.int32)
    for r in range(requests):
        length_ref[r] = length[r, 0]
        offsets_ref[r] = starts[r][0, 0] + before
        next_ref[r] = chosen[r, 0]

    keep.wait()

    arrived(incoming, devices - 1, row_recv)
    rows = incoming[...].reshape(devices * FOLD, slab)
    placed = jnp.dot(placing, rows, preferred_element_type=jnp.float32).astype(jnp.bfloat16)
    for part in range(FOLD):
        dest_ref[:, part * slab : (part + 1) * slab] = placed[part * block : (part + 1) * block, :]

    arrived(counts, devices - 1, count_send)
    arrived(incoming, devices - 1, row_send)


def hand_on(*refs):
    half = (len(refs) - 1) // 2
    sems = refs[-1]
    copies = [pltpu.make_async_copy(refs[i], refs[half + i], sems.at[i]) for i in range(half)]
    for copy in copies:
        copy.start()
    for copy in copies:
        copy.wait()


def solution(mesh):
    n_gx, n_gy = mesh.shape["gx"], mesh.shape["gy"]
    devices = n_gx * n_gy

    def local(hidden, parents, accepted, token_ids):
        requests, nodes, width = hidden.shape
        block = requests * DEPTH
        slab = width // FOLD
        vmem = pl.BlockSpec(memory_space=pltpu.VMEM)
        smem = pl.BlockSpec(memory_space=pltpu.SMEM)
        small = jax.ShapeDtypeStruct((requests,), jnp.int32)
        anywhere = pl.BlockSpec(memory_space=pl.ANY)
        outs = (jax.ShapeDtypeStruct((block, width), hidden.dtype), small, small, small)
        results = pl.pallas_call(
            functools.partial(kernel, (n_gx, n_gy, requests, nodes, width, block)),
            out_shape=outs,
            in_specs=[pl.BlockSpec(memory_space=pltpu.HBM)] * 4,
            out_specs=(vmem, smem, smem, smem),
            scratch_shapes=[
                pltpu.VMEM(hidden.shape, hidden.dtype),
                pltpu.VMEM((requests, nodes), jnp.int32),
                pltpu.VMEM((requests, nodes), jnp.int32),
                pltpu.VMEM((requests, nodes), jnp.int32),
                pltpu.VMEM((block + 1, FOLD, slab), hidden.dtype),
                pltpu.VMEM((devices, FOLD, slab), hidden.dtype),
                pltpu.VMEM((devices, FOLD, slab), hidden.dtype),
                pltpu.VMEM((1, 1, 128), jnp.int32),
                pltpu.VMEM((devices, 1, 128), jnp.int32),
                pltpu.SemaphoreType.DMA,
                pltpu.SemaphoreType.DMA((3,)),
                pltpu.SemaphoreType.DMA,
                pltpu.SemaphoreType.DMA,
                pltpu.SemaphoreType.DMA,
                pltpu.SemaphoreType.DMA,
                pltpu.SemaphoreType.DMA,
            ],
            compiler_params=pltpu.CompilerParams(
                collective_id=0, has_side_effects=True, vmem_limit_bytes=24 << 20
            ),
        )(*[pltpu.with_memory_space_constraint(x, pltpu.HBM) for x in (hidden, parents, accepted, token_ids)])
        return pl.pallas_call(
            hand_on,
            out_shape=outs,
            in_specs=[anywhere] * len(outs),
            out_specs=(anywhere,) * len(outs),
            scratch_shapes=[pltpu.SemaphoreType.DMA((len(outs),))],
            compiler_params=pltpu.CompilerParams(vmem_limit_bytes=1 << 20),
        )(*results)

    placed = (
        P(("gx", "gy"), None, None),
        P(("gx", "gy"), None),
        P(("gx", "gy"), None),
        P(("gx", "gy"), None),
    )
    return jax.shard_map(
        local,
        mesh=mesh,
        in_specs=placed,
        out_specs=(P(("gx", "gy"), None), P(("gx", "gy")), P(("gx", "gy")), P(("gx", "gy"))),
        check_vma=False,
    )
```
